256 devices in a mesh: prompt: 8 (over x_lo, y), resp: 32 (over x_hi, z, core).
Axes of the slice: x: 4 (x_hi: 2, x_lo: 2; x = x_hi * 2 + x_lo), y: 4, z: 8, core: 2. Of those that a mesh axis runs over, the one named last changes fastest.
Arguments:
- question_key_matrix: bfloat16 [32, 2048, 256], P('resp', 'prompt'), may hold values from -0.31835938 to 0.31835938
- prompt_values: bfloat16 [32, 2048, 256], P('resp', 'prompt'), may hold values from -6 to 6
- prompt_gates: float32 [32, 2, 2048], P('resp', None, 'prompt'), may hold values from -2.3 to 0, as said below
- resp_queries: bfloat16 [1024, 512, 256], P(('prompt', 'resp')), may hold values from -0.31835938 to 0.31835938
- resp_keys: bfloat16 [1024, 512, 256], P(('prompt', 'resp')), may hold values from -0.31835938 to 0.31835938
- response_value_rows: bfloat16 [1024, 512, 256], P(('prompt', 'resp')), may hold values from -6 to 6
- resp_gates: float32 [1024, 2, 512], P(('prompt', 'resp')), may hold values from -2.3 to 0, as said below
- resp_cotangent: bfloat16 [1024, 512, 256], P(('prompt', 'resp')), may hold values from -0.59765625 to 0.59765625
- group_ids: int32 [1024], P(('prompt', 'resp')), may hold values from 0 to 31, as said below
- resp_lengths: int32 [256, 4], P(('prompt', 'resp')), may hold values from 1 to 512, 1536 in all within a row
- loss_mask: int32 [1024, 512], P(('prompt', 'resp')), may hold values 0 or 1
- advantages: int32 [1024], P(('prompt', 'resp')), may hold values from -2048 to 2048
Outputs:
- resp_out: bfloat16 [1024, 512, 256], P(('prompt', 'resp'))
- resp_dq: bfloat16 [1024, 512, 256], P(('prompt', 'resp'))
- answer_key_derivative: bfloat16 [1024, 512, 256], P(('prompt', 'resp'))
- resp_dv: bfloat16 [1024, 512, 256], P(('prompt', 'resp'))
- prompt_dk: bfloat16 [32, 2048, 256], P('resp', 'prompt')
- prompt_dv: bfloat16 [32, 2048, 256], P('resp', 'prompt')
The draws below stay inside these ranges and needn't reach their ends.
Inputs may be any that keep to these rules, and one draw needn't show every extreme that they name: `group_ids`: never falling along the responses; every prompt has at least one response. `resp_lengths`: the lengths of one device's 4 responses sum to 1536. `prompt_gates`: negative log decays. `resp_gates`: negative log decays.
All inputs are finite; a program needn't handle non-finite values. No bound on the sum of `loss_mask` on one device may be relied on, other than what follows from the above.
Results may differ from the reference program's by a relative error of at most 0.012.
Values may be sent and summed in bfloat16 or wider, within the bound.
A program may use at most 64 MiB of HBM per device.

```python
import math
import jax
import jax.numpy as jnp
import numpy as np
from jax import lax

H = 2
DH = 128
RMAX = 512
RESP_DEV = 4
NPR = 32
PLEN = 2048
NRESP = 1024
LIVE_DEV = 1536
N_PROMPT = 8
N_RESP = 32


def gate_law(key, rows, token_count):
    keys_all = jax.random.split(key, 4)
    slow_head = jax.random.randint(keys_all[0], (rows, 1), 0, H)
    slow = jnp.arange(H)[None, :] == slow_head
    factor = jnp.exp(jax.random.uniform(keys_all[1], (rows, H, token_count), jnp.float32, -0.7, 0.7))
    slow_rate = math.log(10.0) / (4.0 * token_count)
    fading_multiplier = jnp.where(slow[:, :, None], slow_rate, 1.0 / 40.0) * factor
    place_indices = jax.random.randint(keys_all[2], (rows, H, 3), 0, token_count)
    discarded_places = jnp.log(jax.random.uniform(keys_all[3], (rows, H, 3), jnp.float32, 0.5, 0.8))
    cohort_batch = jnp.sum(jnp.where(place_indices[..., None] == jnp.arange(token_count), discarded_places[..., None], 0.0), axis=2)
    return (cohort_batch - fading_multiplier).astype(jnp.float32)


def draw_prompt_gates(key, part):
    return gate_law(key, NPR, PLEN)


def draw_resp_gates(key, part):
    return gate_law(key, NRESP, RMAX)


def draw_group_ids(key, part):
    base = jnp.arange(NPR, dtype=jnp.int32)
    extra = jax.random.randint(key, (NRESP - NPR,), 0, NPR, dtype=jnp.int32)
    return jnp.sort(jnp.concatenate([base, extra]))


def plant(array, rng, least, largest):
    longest = array.shape.index(max(array.shape))
    spots = []
    for shift in (0, 1):
        where = [jax.random.randint(jax.random.fold_in(rng, axis), (), 0, length) for axis, length in enumerate(array.shape)]
        where[longest] = (where[longest] + shift) % array.shape[longest]
        spots.append(tuple(where))
    return array.at[spots[0]].set(least).at[spots[1]].set(largest)


def shard_levels(rng, extent, cuts, low, largest):
    gain = 1.0
    for axis_at, parts in cuts:
        draws = jax.random.uniform(jax.random.fold_in(jax.random.fold_in(rng, 6), axis_at), (parts,), jnp.float32, low / len(cuts), largest / len(cuts))
        gain = gain * jnp.repeat(jnp.exp(draws), extent[axis_at] // parts).reshape((-1,) + (1,) * (len(extent) - 1 - axis_at))
    return gain


def profile(amount, total, limit, lean):
    weights = [(1 << 20) // math.isqrt(grade ** lean) + 1 for grade in range(2, amount + 1)]
    spare, counts = total - limit - (amount - 1), [1] * (amount - 1)
    while spare > 0:
        candidates = [i for i in range(amount - 1) if counts[i] < limit]
        whole, budget = sum([weights[i] for i in candidates]), spare
        for i in candidates:
            addition = min(limit - counts[i], max(1, budget * weights[i] // whole), spare)
            counts[i] = counts[i] + addition
            spare = spare - addition
    return np.array([limit] + counts)


def ragged_sizes(key, amount, total, limit, skew):
    if amount == 2:
        one = jax.random.randint(key, (), max(1, total - limit), min(limit, total - 1) + 1)
        return jnp.stack([one, total - one])
    tallies = jnp.asarray(profile(amount, total, limit, skew), jnp.int32)
    couples = (amount - 1) // 2
    source_of, taker = tallies[1:1 + 2 * couples:2], tallies[2:2 + 2 * couples:2]
    room = jnp.minimum(source_of - 1, limit - taker)
    moved = jax.random.randint(jax.random.fold_in(key, 1), (couples,), 0, 1 << 20) % (room + 1)
    tallies = tallies.at[1:1 + 2 * couples:2].set(source_of - moved).at[2:2 + 2 * couples:2].set(taker + moved)
    return tallies[jax.random.permutation(jax.random.fold_in(key, 2), amount)]


def noise(key, extent, scale, limit, cuts=(), kind=jnp.bfloat16):
    values = jax.random.normal(key, extent, jnp.float32) * scale
    if len(cuts) > 0:
        values = shard_levels(key, extent, cuts, -0.22, 0.18) * values
    return jnp.clip(values, min=-limit, max=limit).astype(kind)


def setup_inputs(seed: int = 0) -> dict:
    key_list = jax.random.split(jax.random.key(seed), 13)
    question_key_matrix = noise(key_list[0], (NPR, PLEN, H * DH), 0.053, 0.31835938, ((0, 32), (1, 8)))
    prompt_values = noise(key_list[1], (NPR, PLEN, H * DH), 1.0, 6.0, ((0, 32), (1, 8)))
    prompt_gates = draw_prompt_gates(jax.random.fold_in(key_list[12], 71), 0)
    resp_queries = noise(key_list[3], (NRESP, RMAX, H * DH), 0.053, 0.31835938, ((0, 256),))
    resp_keys = noise(key_list[4], (NRESP, RMAX, H * DH), 0.053, 0.31835938, ((0, 256),))
    response_value_rows = noise(key_list[5], (NRESP, RMAX, H * DH), 1.0, 6.0, ((0, 256),))
    resp_gates = draw_resp_gates(jax.random.fold_in(key_list[12], 71), 0)
    resp_cotangent = noise(key_list[7], (NRESP, RMAX, H * DH), 0.1, 0.59765625, ((0, 256),))
    group_ids = draw_group_ids(jax.random.fold_in(key_list[12], 71), 0)
    resp_lengths = jax.vmap(lambda own: ragged_sizes(own, RESP_DEV, LIVE_DEV, RMAX, 2))(jax.random.split(key_list[9], (N_PROMPT * N_RESP))).reshape((N_PROMPT * N_RESP, RESP_DEV)).astype(jnp.int32)
    loss_mask = plant((jax.random.randint(key_list[10], (NRESP, RMAX), 0, 4) < 3).astype(jnp.int32), jax.random.fold_in(key_list[10], 1), 0, 1)
    advantages = plant(jax.random.randint(key_list[11], (NRESP,), -2048, 2049), jax.random.fold_in(key_list[11], 1), -2048, 2048).astype(jnp.int32)
    return dict(question_key_matrix=question_key_matrix, prompt_values=prompt_values, prompt_gates=prompt_gates, resp_queries=resp_queries, resp_keys=resp_keys, response_value_rows=response_value_rows, resp_gates=resp_gates, resp_cotangent=resp_cotangent, group_ids=group_ids, resp_lengths=resp_lengths, loss_mask=loss_mask, advantages=advantages)


def head_pass(query_h, key_h, value_h, gate_h, start_h, cot_h, weight, live_rows, open_rows):
    cum_gate = jnp.cumsum(gate_h)
    places = jnp.arange(gate_h.shape[0])
    causal = places[:, None] >= places[None, :]
    decay = jnp.where(causal, jnp.exp(jnp.where(causal, cum_gate[:, None] - cum_gate[None, :], 0.0)), 0.0)
    carried = jnp.exp(cum_gate)[:, None]
    start_b = start_h.astype(jnp.bfloat16)
    scores = jnp.dot(query_h, key_h.T, preferred_element_type=jnp.float32)
    mixing = (scores * decay).astype(jnp.bfloat16)
    output = carried * jnp.dot(query_h, start_b, preferred_element_type=jnp.float32)
    output = (output + jnp.dot(mixing, value_h, preferred_element_type=jnp.float32)) * open_rows[:, None]
    grad_out = (cot_h.astype(jnp.float32) * (live_rows * weight)[:, None]).astype(jnp.bfloat16)
    grad_mix = jnp.dot(grad_out, value_h.T, preferred_element_type=jnp.float32)
    grad_scores = (grad_mix * decay).astype(jnp.bfloat16)
    grad_query = jnp.dot(grad_scores, key_h, preferred_element_type=jnp.float32)
    grad_query = grad_query + carried * jnp.dot(grad_out, start_b.T, preferred_element_type=jnp.float32)
    grad_key = jnp.dot(grad_scores.T, query_h, preferred_element_type=jnp.float32)
    grad_value = jnp.dot(mixing.T, grad_out, preferred_element_type=jnp.float32)
    scaled_out = (carried * grad_out.astype(jnp.float32)).astype(jnp.bfloat16)
    opening_memory_derivative = jnp.dot(query_h.T, scaled_out, preferred_element_type=jnp.float32)
    return output, grad_query, grad_key, grad_value, opening_memory_derivative


def response_sweep(queries, keys_in, values, gates, start, cotangent, weight, live_rows, open_rows):
    width = start.shape[1]
    pieces = []
    for head_index in range(start.shape[0]):
        lower = head_index * width
        upper = lower + width
        pieces.append(head_pass(queries[:, lower:upper], keys_in[:, lower:upper], values[:, lower:upper],
                                gates[head_index], start[head_index], cotangent[:, lower:upper],
                                weight, live_rows, open_rows))
    joined = [jnp.concatenate([entry[slot] for entry in pieces], axis=1).astype(jnp.bfloat16) for slot in range(4)]
    opening_memory_derivative = jnp.stack([entry[4] for entry in pieces])
    return joined[0], joined[1], joined[2], joined[3], opening_memory_derivative


def prompt_state(keys_in, values, gates):
    width = keys_in.shape[1] // gates.shape[0]
    states = []
    for head_index in range(gates.shape[0]):
        lower = head_index * width
        suffix = jnp.cumsum(gates[head_index][::-1])[::-1] - gates[head_index]
        key_f = keys_in[:, lower:lower + width].astype(jnp.float32)
        value_f = values[:, lower:lower + width].astype(jnp.float32)
        states.append(jnp.dot(key_f.T, jnp.exp(suffix)[:, None] * value_f, precision=lax.Precision.HIGHEST))
    return jnp.stack(states)


def prompt_grads(keys_in, values, gates, grad_state):
    width = keys_in.shape[1] // gates.shape[0]
    grad_keys = []
    grad_values = []
    for head_index in range(gates.shape[0]):
        lower = head_index * width
        suffix = jnp.cumsum(gates[head_index][::-1])[::-1] - gates[head_index]
        factor = jnp.exp(suffix)[:, None]
        key_f = keys_in[:, lower:lower + width].astype(jnp.float32)
        value_f = values[:, lower:lower + width].astype(jnp.float32)
        grad_keys.append(factor * jnp.dot(value_f, grad_state[head_index].T, precision=lax.Precision.HIGHEST))
        grad_values.append(factor * jnp.dot(key_f, grad_state[head_index], precision=lax.Precision.HIGHEST))
    return (jnp.concatenate(grad_keys, axis=1).astype(jnp.bfloat16),
            jnp.concatenate(grad_values, axis=1).astype(jnp.bfloat16))


def reference(question_key_matrix, prompt_values, prompt_gates, resp_queries, resp_keys, response_value_rows, resp_gates,
              resp_cotangent, group_ids, resp_lengths, loss_mask, advantages):
    def state_item(item):
        return prompt_state(item[0], item[1], item[2])

    states = lax.map(state_item, (question_key_matrix, prompt_values, prompt_gates))
    lengths = resp_lengths.reshape(-1)
    places = jnp.arange(RMAX)
    open_rows = (places[None, :] < lengths[:, None]).astype(jnp.float32)
    live_rows = loss_mask.astype(jnp.float32) * open_rows
    weights = advantages.astype(jnp.float32) / 1024.0

    def resp_item(item):
        start = lax.dynamic_index_in_dim(states, item[5].astype(jnp.int32), 0, keepdims=False)
        return response_sweep(item[0], item[1], item[2], item[3], start, item[4], item[6], item[7], item[8])

    outs = lax.map(resp_item, (resp_queries, resp_keys, response_value_rows, resp_gates, resp_cotangent,
                               group_ids, weights, live_rows, open_rows))
    grad_final = jax.ops.segment_sum(outs[4], group_ids, num_segments=NPR)

    def grad_item(item):
        return prompt_grads(item[0], item[1], item[2], item[3])

    prompt_dk, prompt_dv = lax.map(grad_item, (question_key_matrix, prompt_values, prompt_gates, grad_final))
    return (outs[0], outs[1], outs[2], outs[3], prompt_dk, prompt_dv)
```

```python
import functools

import jax
import jax.numpy as jnp
from jax import lax
from jax.experimental import pallas as pl
from jax.experimental.pallas import tpu as pltpu
from jax.sharding import PartitionSpec as P

H = 2
DH = 128
RMAX = 512
NR = 4
PIECE = 256
PLANE = 32
RING = 8
CH = 256
HI = lax.Precision.HIGHEST
MESH = pl.DeviceIdType.MESH
F32 = jnp.float32
BF16 = jnp.bfloat16


def mm(x, y, cx, cy, **kw):
    return lax.dot_general(x, y, (((cx,), (cy,)), ((), ())), preferred_element_type=F32, **kw)


def split(x):
    hi = x.astype(BF16)
    return hi, (x - hi.astype(F32)).astype(BF16)


def iota(shape, axis):
    return lax.broadcasted_iota(jnp.int32, shape, axis)


def exchange_kernel(
    gid, lens, adv, pk_hbm, pv_hbm, pg, q_hbm, cot_hbm, rg, mask,
    dk_out, dv_out, starts_out,
    pk, pv, q, cot, f1s, f1r, f2s, f2r, f3s, f3r, g1s, g1r, g2s, g2r, g3s, g3r, oh,
    in_sems, send_sems, recv_sems,
):
    a = lax.axis_index("prompt")
    b = lax.axis_index("resp")
    quad = lax.div(b, 16) * 2 + lax.rem(b, 2)
    z = lax.rem(lax.div(b, 2), RING)
    me = a * 4 + quad

    def plane_peer(k):
        j = lax.rem(me + k, PLANE)
        qj = lax.rem(j, 4)
        return j, (lax.div(j, 4), lax.div(qj, 2) * 16 + z * 2 + lax.rem(qj, 2))

    def ring_peer(k):
        zz = lax.rem(z + k, RING)
        return zz, (a, lax.div(quad, 2) * 16 + zz * 2 + lax.rem(quad, 2))

    loads = [
        pltpu.make_async_copy(s, d, in_sems.at[i])
        for i, (s, d) in enumerate(((pk_hbm, pk), (pv_hbm, pv), (q_hbm, q), (cot_hbm, cot)))
    ]
    for c in loads:
        c.start()

    barrier = pltpu.get_barrier_semaphore()

    def greet_plane(k, _):
        pl.semaphore_signal(barrier, inc=1, device_id=plane_peer(k)[1], device_id_type=MESH)
        return 0

    def greet_ring(k, _):
        pl.semaphore_signal(barrier, inc=1, device_id=ring_peer(k)[1], device_id_type=MESH)
        return 0

    lax.fori_loop(1, PLANE, greet_plane, 0)
    lax.fori_loop(1, RING, greet_ring, 0)

    def send_all(n, peer, stage, src_of, dst):
        def one(k, _):
            j, dev = peer(k)
            pltpu.make_async_remote_copy(
                src_ref=src_of(j),
                dst_ref=dst,
                send_sem=send_sems.at[stage],
                recv_sem=recv_sems.at[stage],
                device_id=dev,
                device_id_type=MESH,
            ).start()
            return 0

        lax.fori_loop(1, n, one, 0)

    def wait_all(ref, sems, stage):
        pltpu.make_async_copy(ref, ref, sems.at[stage]).wait()

    gates = jnp.concatenate([pg[0], jnp.zeros((6, PIECE), F32)], axis=0)
    later = (iota((PIECE, PIECE), 1) > iota((PIECE, PIECE), 0)).astype(F32)
    suf = mm(later, gates, 1, 1, precision=HI)
    total = jnp.sum(gates, axis=1, keepdims=True)
    loads[0].wait()
    loads[1].wait()
    for h in range(H):
        cols = slice(h * DH, (h + 1) * DH)
        hi, lo = split(jnp.exp(suf[:, h : h + 1]) * pv[0, :, cols].astype(F32))
        kh = pk[0, :, cols]
        state = mm(kh, hi, 0, 0) + mm(kh, lo, 0, 0)
        f1s[h * 16 : (h + 1) * 16, 0:8, :] = state.reshape(16, 8, DH)
    row = iota((8, DH), 0)
    meta = jnp.broadcast_to(total, (8, DH))
    for r in range(NR):
        g = gid[r]
        slot = ((g >> 1) & 7) * 4 + (g >> 4) * 2 + (g & 1)
        meta = jnp.where(row == 2 + r, (slot * 8).astype(F32), meta)
    f1s[:, 8:16, :] = jnp.broadcast_to(meta[None], (PLANE, 8, DH))
    f1r[me] = f1s[me]

    pl.semaphore_wait(barrier, PLANE - 1 + RING - 1)
    send_all(PLANE, plane_peer, 0, lambda j: f1s.at[j], f1r.at[me])

    upper = (iota((DH, DH), 0) <= iota((DH, DH), 1)).astype(F32)
    nch = RMAX // DH
    grows = jnp.concatenate(
        [rg[r, :, c * DH : (c + 1) * DH] for c in range(nch) for r in range(NR)], axis=0
    )
    grows = mm(grows, upper, 1, 0, precision=HI)
    before = jnp.zeros((8, 1), F32)
    erows = []
    for c in range(nch):
        local = grows[c * 8 : (c + 1) * 8]
        erows.append(jnp.exp(local + before))
        before = before + local[:, DH - 1 : DH]
    lane = iota((1, DH), 1)
    lrows = []
    for c in range(nch):
        for r in range(NR):
            on = mask[r : r + 1, c * DH : (c + 1) * DH].astype(F32)
            on = jnp.where(lane + c * DH < lens[0, r], on, 0.0)
            lrows.append(on * (adv[r].astype(F32) * (1.0 / 1024.0)))
    rows = jnp.concatenate(erows + lrows + [jnp.zeros((DH - 48, DH), F32)], axis=0)
    columns = rows.T
    loads[2].wait()
    loads[3].wait()
    for pair in range(NR // 2):
        for h in range(H):
            cols = slice(h * DH, (h + 1) * DH)
            found = []
            for r in (2 * pair, 2 * pair + 1):
                parts = []
                for c in range(nch):
                    live = columns[:, 32 + c * 4 + r : 33 + c * 4 + r]
                    e = columns[:, c * 8 + r * 2 + h : c * 8 + r * 2 + h + 1]
                    go = cot[r, c * DH : (c + 1) * DH, cols].astype(F32) * live
                    parts.append((go.astype(BF16).astype(F32) * e).astype(BF16))
                scaled = jnp.concatenate(parts, axis=0)
                found.append(mm(q[r, :, cols], scaled, 0, 0).reshape(16, 8, DH))
            g1s[h * 16 : (h + 1) * 16, pair * 16 : (pair + 1) * 16, :] = jnp.concatenate(
                found, axis=1
            ).astype(BF16)
    g1r[me] = g1s[me]
    send_all(PLANE, plane_peer, 3, lambda j: g1s.at[j], g1r.at[me])

    wait_all(f1r.at[pl.ds(0, PLANE - 1)], recv_sems, 0)
    data = f1r[:, 0:8, :].reshape(8, 4, 8, DH)
    logs = jnp.where(a >= 4, f1r[:, 9:10, :], f1r[:, 8:9, :]).reshape(8, 4, 1, DH)
    acc = data[7]
    run = logs[7]
    for piece in range(6, -1, -1):
        acc = acc + jnp.exp(run) * data[piece]
        run = run + logs[piece]
    f2s[...] = acc.reshape(32, DH).astype(BF16)
    f2r[z] = f2s[...]
    send_all(RING, ring_peer, 1, lambda j: f2s, f2r.at[z])

    after = jnp.zeros((8, DH), F32)
    for piece in range(8):
        after = after + jnp.where(piece > a, f1r[piece * 4 + quad, 8:16, :], 0.0)
    sub = iota((1, 8, DH), 1).astype(F32)
    wide = jnp.concatenate(
        [jnp.broadcast_to(f1r[:, 10 + r : 11 + r, :], (PLANE, 8, DH)) + sub for r in range(NR)], axis=1
    ).reshape(PLANE * 32, DH)
    lanes = iota((1, DH), 1).astype(F32)
    oh[:, 0:DH] = jnp.where(wide == lanes, 1.0, 0.0).astype(BF16)
    oh[:, DH : 2 * DH] = jnp.where(wide == lanes + float(DH), 1.0, 0.0).astype(BF16)

    wait_all(g1r.at[pl.ds(0, PLANE - 1)], recv_sems, 3)
    added = mm(oh[...], g1r[...].reshape(PLANE * 32, DH), 0, 0)
    g2s[...] = added.astype(BF16).reshape(RING, 32, DH)
    g2r[z] = g2s[z]
    send_all(RING, ring_peer, 4, lambda j: g2s.at[j], g2r.at[z])

    wait_all(f2r.at[pl.ds(0, RING - 1)], recv_sems, 1)
    picked = mm(oh[...], f2r[...].reshape(RING * 32, DH), 1, 0)
    f3s[...] = picked.astype(BF16).reshape(PLANE, 32, DH)
    f3r[me] = f3s[me]
    send_all(PLANE, plane_peer, 2, lambda j: f3s.at[j], f3r.at[me])

    wait_all(g2r.at[pl.ds(0, RING - 1)], recv_sems, 4)
    g3s[...] = jnp.sum(g2r[...].astype(F32), axis=0).reshape(4, 8, DH)
    g3r[me] = g3s[quad]
    send_all(PLANE, plane_peer, 5, lambda j: g3s.at[lax.rem(j, 4)], g3r.at[me])

    wait_all(g3r.at[pl.ds(0, PLANE - 1)], recv_sems, 5)
    for h in range(H):
        cols = slice(h * DH, (h + 1) * DH)
        factor = jnp.exp(suf[:, h : h + 1] + after[h : h + 1, 0:1])
        hi, lo = split(g3r[h * 16 : (h + 1) * 16].reshape(DH, DH))
        vh = pv[0, :, cols]
        kh = pk[0, :, cols]
        dk_out[0, :, cols] = (factor * (mm(vh, hi, 1, 1) + mm(vh, lo, 1, 1))).astype(BF16)
        dv_out[0, :, cols] = (factor * (mm(kh, hi, 1, 0) + mm(kh, lo, 1, 0))).astype(BF16)

    wait_all(f3r.at[pl.ds(0, PLANE - 1)], recv_sems, 2)
    got = f3r[...].astype(F32)
    for r in range(NR):
        starts_out[r] = got[:, r * 8 : (r + 1) * 8, :].reshape(2 * DH, DH).astype(BF16)

    wait_all(f1s.at[pl.ds(0, PLANE - 1)], send_sems, 0)
    wait_all(f2r.at[pl.ds(0, RING - 1)], send_sems, 1)
    wait_all(f3s.at[pl.ds(0, PLANE - 1)], send_sems, 2)
    wait_all(g1s.at[pl.ds(0, PLANE - 1)], send_sems, 3)
    wait_all(g2s.at[pl.ds(0, RING - 1)], send_sems, 4)
    wait_all(g3r.at[pl.ds(0, PLANE - 1)], send_sems, 5)


def exchange(gid, lens, adv, pk, pv, pg, q, cot, rg, mask):
    smem = pl.BlockSpec(memory_space=pltpu.SMEM)
    vmem = pl.BlockSpec(memory_space=pltpu.VMEM)
    anywhere = pl.BlockSpec(memory_space=pl.ANY)
    return pl.pallas_call(
        exchange_kernel,
        out_shape=(
            jax.ShapeDtypeStruct((1, PIECE, H * DH), BF16),
            jax.ShapeDtypeStruct((1, PIECE, H * DH), BF16),
            jax.ShapeDtypeStruct((NR, H * DH, DH), BF16),
        ),
        in_specs=[smem, smem, smem, anywhere, anywhere, vmem, anywhere, anywhere, vmem, vmem],
        out_specs=(vmem, vmem, vmem),
        scratch_shapes=[
            pltpu.VMEM((1, PIECE, H * DH), BF16),
            pltpu.VMEM((1, PIECE, H * DH), BF16),
            pltpu.VMEM((NR, RMAX, H * DH), BF16),
            pltpu.VMEM((NR, RMAX, H * DH), BF16),
            pltpu.VMEM((PLANE, 16, DH), F32),
            pltpu.VMEM((PLANE, 16, DH), F32),
            pltpu.VMEM((32, DH), BF16),
            pltpu.VMEM((RING, 32, DH), BF16),
            pltpu.VMEM((PLANE, 32, DH), BF16),
            pltpu.VMEM((PLANE, 32, DH), BF16),
            pltpu.VMEM((PLANE, 32, DH), BF16),
            pltpu.VMEM((PLANE, 32, DH), BF16),
            pltpu.VMEM((RING, 32, DH), BF16),
            pltpu.VMEM((RING, 32, DH), BF16),
            pltpu.VMEM((4, 8, DH), F32),
            pltpu.VMEM((PLANE, 8, DH), F32),
            pltpu.VMEM((PLANE * 32, 2 * DH), BF16),
            pltpu.SemaphoreType.DMA((4,)),
            pltpu.SemaphoreType.DMA((6,)),
            pltpu.SemaphoreType.DMA((6,)),
        ],
        compiler_params=pltpu.CompilerParams(
            collective_id=0, has_side_effects=True, vmem_limit_bytes=32 << 20
        ),
        name="exchange",
    )(gid, lens, adv, pk, pv, pg, q, cot, rg, mask)


def response_kernel(lens, adv, q_ref, k_ref, v_ref, cot_ref, rg, mask, start_ref, out_ref, dq_ref, dk_ref, dv_ref):
    r = pl.program_id(0)
    length = lens[0, r]
    weight = adv[r].astype(F32) * (1.0 / 1024.0)
    nch = RMAX // CH

    def body(chunks):
        upper = (iota((CH, CH), 0) <= iota((CH, CH), 1)).astype(F32)
        lane = iota((1, CH), 1)
        grows = jnp.concatenate(
            [rg[0, :, c * CH : (c + 1) * CH] for c in range(nch)] + [jnp.zeros((8 - 2 * nch, CH), F32)],
            axis=0,
        )
        crows = mm(grows, upper, 1, 0, precision=HI)
        lrows = []
        for c in range(nch):
            on = mask[pl.ds(r, 1), c * CH : (c + 1) * CH].astype(F32)
            lrows.append(jnp.where(lane + c * CH < length, on, 0.0) * weight)
        rows = jnp.concatenate([crows] + lrows + [jnp.zeros((DH - 8 - nch, CH), F32)], axis=0)
        columns = rows.T
        causal = iota((CH, CH), 0) >= iota((CH, CH), 1)
        place = iota((CH, 1), 0)
        for h in range(H):
            cols = slice(h * DH, (h + 1) * DH)
            state = start_ref[0, cols, :]
            q, k, v, go, col, tot = [], [], [], [], [], []
            for c in range(chunks):
                tok = slice(c * CH, (c + 1) * CH)
                q.append(q_ref[0, tok, cols])
                k.append(k_ref[0, tok, cols])
                v.append(v_ref[0, tok, cols])
                live = columns[:, 8 + c : 9 + c]
                go.append((cot_ref[0, tok, cols].astype(F32) * live).astype(BF16))
                col.append(columns[:, 2 * c + h : 2 * c + h + 1])
                tot.append(crows[2 * c + h : 2 * c + h + 1, CH - 1 : CH])
            back = [None] * chunks
            for c in range(chunks - 1, 0, -1):
                scaled = (jnp.exp(col[c]) * go[c].astype(F32)).astype(BF16)
                grad = mm(q[c], scaled, 0, 0)
                if back[c] is not None:
                    grad = grad + jnp.exp(tot[c]) * back[c]
                back[c - 1] = grad
            for c in range(chunks):
                tok = slice(c * CH, (c + 1) * CH)
                e = jnp.exp(col[c])
                f = jnp.exp(tot[c] - col[c])
                decay = jnp.exp(
                    jnp.where(causal, col[c] - crows[2 * c + h : 2 * c + h + 1, :], -1e30)
                )
                mix = (mm(q[c], k[c], 1, 1) * decay).astype(BF16)
                gs = (mm(go[c], v[c], 1, 1) * decay).astype(BF16)
                sb = state.astype(BF16)
                out = e * mm(q[c], sb, 1, 0) + mm(mix, v[c], 1, 0)
                out_ref[0, tok, cols] = jnp.where(place + c * CH < length, out, 0.0).astype(BF16)
                dq_ref[0, tok, cols] = (e * mm(go[c], sb, 1, 1) + mm(gs, k[c], 1, 0)).astype(BF16)
                dk = mm(gs, q[c], 0, 0)
                dv = mm(mix, go[c], 0, 0)
                if back[c] is not None:
                    bb = back[c].astype(BF16)
                    dk = dk + f * mm(v[c], bb, 1, 1)
                    dv = dv + f * mm(k[c], bb, 1, 0)
                dk_ref[0, tok, cols] = dk.astype(BF16)
                dv_ref[0, tok, cols] = dv.astype(BF16)
                if c + 1 < chunks:
                    vf = (f * v[c].astype(F32)).astype(BF16)
                    state = jnp.exp(tot[c]) * state.astype(F32) + mm(k[c], vf, 0, 0)
        for c in range(chunks, nch):
            tok = slice(c * CH, (c + 1) * CH)
            for ref in (out_ref, dq_ref, dk_ref, dv_ref):
                ref[0, tok, :] = jnp.zeros((CH, H * DH), BF16)

    for n in range(1, nch + 1):
        low = (n - 1) * CH
        cond = length > low if n == nch else jnp.logical_and(length > low, length <= n * CH)
        pl.when(cond)(functools.partial(body, n))


def response(lens, adv, q, k, v, cot, rg, mask, starts):
    smem = pl.BlockSpec(memory_space=pltpu.SMEM)
    big = pl.BlockSpec((1, RMAX, H * DH), lambda r: (r, 0, 0))
    shape = jax.ShapeDtypeStruct((NR, RMAX, H * DH), BF16)
    return pl.pallas_call(
        response_kernel,
        grid=(NR,),
        out_shape=(shape,) * 4,
        in_specs=[
            smem,
            smem,
            big,
            big,
            big,
            big,
            pl.BlockSpec((1, H, RMAX), lambda r: (r, 0, 0)),
            pl.BlockSpec((NR, RMAX), lambda r: (0, 0)),
            pl.BlockSpec((1, H * DH, DH), lambda r: (r, 0, 0)),
        ],
        out_specs=(big,) * 4,
        compiler_params=pltpu.CompilerParams(
            dimension_semantics=("arbitrary",), vmem_limit_bytes=48 << 20
        ),
        name="response",
    )(lens, adv, q, k, v, cot, rg, mask, starts)


def shards(pk, pv, pg, q, k, v, rg, cot, gid, lens, mask, adv):
    dk, dv, starts = exchange(gid, lens, adv, pk, pv, pg, q, cot, rg, mask)
    out, dq, rdk, rdv = response(lens, adv, q, k, v, cot, rg, mask, starts)
    return out, dq, rdk, rdv, dk, dv


def solution(mesh):
    both = ("prompt", "resp")
    pieces = P("resp", "prompt", None)
    slots = P(both, None, None)
    return jax.shard_map(
        shards,
        mesh=mesh,
        in_specs=(
            pieces,
            pieces,
            P("resp", None, "prompt"),
            slots,
            slots,
            slots,
            slots,
            slots,
            P(both),
            P(both, None),
            P(both, None),
            P(both),
        ),
        out_specs=(slots, slots, slots, slots, pieces, pieces),
        check_vma=False,
    )
```

```python
import jax
import jax.numpy as jnp
from jax import lax
from jax.experimental import pallas as pl
from jax.experimental.pallas import tpu as pltpu
from jax.sharding import PartitionSpec as P

H = 2
DH = 128
RMAX = 512
NR = 4
PIECE = 256
PLANE = 32
RING = 8
CH = 256
HI = lax.Precision.HIGHEST
MESH = pl.DeviceIdType.MESH
F32 = jnp.float32
BF16 = jnp.bfloat16
HEADS = [slice(h * DH, (h + 1) * DH) for h in range(H)]
TOKENS = [slice(c * CH, (c + 1) * CH) for c in range(RMAX // CH)]


def mm(x, y, cx, cy, **kw):
    return lax.dot_general(x, y, (((cx,), (cy,)), ((), ())), preferred_element_type=F32, **kw)


def split(x):
    hi = x.astype(BF16)
    return hi, (x - hi.astype(F32)).astype(BF16)


def iota(shape, axis):
    return lax.broadcasted_iota(jnp.int32, shape, axis)


def col(cols, r, item):
    return cols[:, r * 16 + item : r * 16 + item + 1]


def exchange_kernel(
    gid_hbm, lens_hbm, adv_hbm, pk_hbm, pv_hbm, pg_hbm, q_hbm, k_hbm, v_hbm, cot_hbm, rg_hbm, mask_hbm,
    pk, pv, q, go, pout, pdq, dk, dv, starts, gfin, cols_out, pfac,
    gid, lens, adv, pg, k, v, rg, mask, crows, cfull, back,
    f1s, f1r, ids, idr, f2s, f2r, f3s, f3r, g1s, g1r, g2s, g2r, g3s, g3r, oh,
    in_sems, send_sems, recv_sems,
):
    a = lax.axis_index("prompt")
    b = lax.axis_index("resp")
    quad = lax.div(b, 16) * 2 + lax.rem(b, 2)
    z = lax.rem(lax.div(b, 2), RING)
    me = a * 4 + quad
    quads = [lax.rem(quad + d, 4) for d in range(4)]
    homes = [lax.div(x, 2) * 16 + z * 2 + lax.rem(x, 2) for x in quads]
    corner = lax.div(b, 16) * 16 + lax.rem(b, 2)
    rings = [lax.rem(z + d, RING) for d in (4, 3, 5, 2, 6, 1, 7)]

    loads = [
        pltpu.make_async_copy(s, d, in_sems.at[i])
        for i, (s, d) in enumerate(
            (
                (pg_hbm, pg), (pk_hbm, pk), (pv_hbm, pv), (gid_hbm, gid), (lens_hbm, lens), (adv_hbm, adv),
                (rg_hbm, rg), (mask_hbm, mask), (cot_hbm, go), (q_hbm, q), (k_hbm, k), (v_hbm, v),
            )
        )
    ]
    for c in loads:
        c.start()

    def to_plane(fn):
        def others(d, _):
            aa = lax.rem(a + d, 8)
            for x, home in zip(quads, homes):
                fn(aa * 4 + x, (aa, home))
            return 0

        lax.fori_loop(1, 8, others, 0)
        for d in (3, 2, 1):
            fn(a * 4 + quads[d], (a, homes[d]))

    def to_ring(fn):
        for zz in rings:
            fn(zz, (a, corner + zz * 2))

    barrier = pltpu.get_barrier_semaphore()

    def greet(_, dev):
        pl.semaphore_signal(barrier, inc=1, device_id=dev, device_id_type=MESH)

    to_plane(greet)
    to_ring(greet)

    def send(stage, src_of, dst):
        def one(j, dev):
            pltpu.make_async_remote_copy(
                src_ref=src_of(j),
                dst_ref=dst,
                send_sem=send_sems.at[stage],
                recv_sem=recv_sems.at[stage],
                device_id=dev,
                device_id_type=MESH,
            ).start()

        return one

    def wait_all(ref, sems, stage):
        pltpu.make_async_copy(ref, ref, sems.at[stage]).wait()

    for c in loads[:6]:
        c.wait()
    gates = jnp.concatenate([pg[0], jnp.zeros((6, PIECE), F32)], axis=0)
    later = (iota((PIECE, PIECE), 1) > iota((PIECE, PIECE), 0)).astype(F32)
    suf = mm(later, gates, 1, 1, precision=HI)
    total = jnp.sum(gates, axis=1, keepdims=True)
    esuf = jnp.exp(suf)
    for h in range(H):
        hi, lo = split(esuf[:, h : h + 1] * pv[0, :, HEADS[h]].astype(F32))
        kh = pk[0, :, HEADS[h]]
        state = mm(kh, hi, 0, 0) + mm(kh, lo, 0, 0)
        f1s[h * 16 : (h + 1) * 16] = state.reshape(16, 8, DH)
    row = iota((8, DH), 0)
    meta = jnp.broadcast_to(total, (8, DH))
    for r in range(NR):
        g = gid[r]
        slot = ((g >> 1) & 7) * 4 + (g >> 4) * 2 + (g & 1)
        meta = jnp.where(row == 2 + r, (slot * 8).astype(F32), meta)
    ids[...] = meta
    f1r[me] = f1s[me]
    idr[me] = meta

    for c in loads[6:8]:
        c.wait()
    upper = (iota((CH, CH), 0) <= iota((CH, CH), 1)).astype(F32)
    lane = iota((1, CH), 1)
    grows = jnp.concatenate([rg[r, :, t] for r in range(NR) for t in TOKENS], axis=0)
    cums = mm(grows, upper, 1, 0, precision=HI)
    crows[...] = cums
    exps = jnp.exp(cums)
    tots = cums[:, CH - 1 : CH]
    falls = jnp.exp(tots - cums)
    rows = []
    for r in range(NR):
        rows += [cums[4 * r : 4 * r + 4], exps[4 * r : 4 * r + 4]]
        opens = [jnp.where(lane + c * CH < lens[0, r], 1.0, 0.0) for c in range(len(TOKENS))]
        for on, t in zip(opens, TOKENS):
            rows.append(on * mask[r : r + 1, t].astype(F32) * (adv[r].astype(F32) * (1.0 / 1024.0)))
        rows += [falls[4 * r : 4 * r + 2]] + opens + [jnp.zeros((2, CH), F32)]
    cols = jnp.concatenate(rows + [jnp.zeros((64, CH), F32)], axis=0).T
    cols_out[...] = cols
    for c in loads[8:10]:
        c.wait()
    for pair in range(NR // 2):
        for h in range(H):
            found = []
            for r in (2 * pair, 2 * pair + 1):
                parts = []
                for c, t in enumerate(TOKENS):
                    grad_out = (go[r, t, HEADS[h]].astype(F32) * col(cols, r, 8 + c)).astype(BF16)
                    go[r, t, HEADS[h]] = grad_out
                    scaled = (grad_out.astype(F32) * col(cols, r, 4 + 2 * c + h)).astype(BF16)
                    parts.append(mm(q[r, t, HEADS[h]], scaled, 0, 0))
                back[r, h] = parts[1].astype(BF16)
                fall = jnp.exp(tots[4 * r + h : 4 * r + h + 1])
                found.append((parts[0] + fall * parts[1]).reshape(16, 8, DH))
            g1s[h * 16 : (h + 1) * 16, pair * 16 : (pair + 1) * 16, :] = jnp.concatenate(
                found, axis=1
            ).astype(BF16)
    g1r[me] = g1s[me]

    pl.semaphore_wait(barrier, PLANE - 1 + RING - 1)
    to_plane(send(0, lambda j: f1s.at[j], f1r.at[me]))
    to_plane(send(6, lambda j: ids, idr.at[me]))
    to_plane(send(3, lambda j: g1s.at[j], g1r.at[me]))

    loads[10].wait()
    loads[11].wait()
    causal = iota((CH, CH), 0) >= iota((CH, CH), 1)

    def inner(r):
        for h in range(H):
            hs = HEADS[h]
            bk = back[r, h]
            step = None
            for c, t in enumerate(TOKENS):
                qc, kc, vc, gc = q[r, t, hs], k[r, t, hs], v[r, t, hs], go[r, t, hs]
                i = 4 * r + 2 * c + h
                decay = jnp.exp(jnp.where(causal, col(cols, r, 2 * c + h) - crows[i : i + 1, :], -1e30))
                mix = (mm(qc, kc, 1, 1) * decay).astype(BF16)
                gs = (mm(gc, vc, 1, 1) * decay).astype(BF16)
                out = mm(mix, vc, 1, 0)
                dq = mm(gs, kc, 1, 0)
                dkc = mm(gs, qc, 0, 0)
                dvc = mm(mix, gc, 0, 0)
                if c == 0:
                    f = col(cols, r, 10 + h)
                    dkc = dkc + f * mm(vc, bk, 1, 1)
                    dvc = dvc + f * mm(kc, bk, 1, 0)
                    step = mm(kc, (f * vc.astype(F32)).astype(BF16), 0, 0).astype(BF16)
                else:
                    e = col(cols, r, 4 + 2 * c + h)
                    out = out + e * mm(qc, step, 1, 0)
                    dq = dq + e * mm(gc, step, 1, 1)
                pout[r, t, hs] = out
                pdq[r, t, hs] = dq
                dk[r, t, hs] = dkc.astype(BF16)
                dv[r, t, hs] = dvc.astype(BF16)

    inner(0)
    inner(1)
    inner(2)

    wait_all(f1r.at[pl.ds(0, PLANE - 1)], recv_sems, 0)
    wait_all(idr.at[pl.ds(0, PLANE - 1)], recv_sems, 6)
    data = f1r[...].reshape(8, 4, 8, DH)
    logs = jnp.where(a >= 4, idr[:, 1:2, :], idr[:, 0:1, :]).reshape(8, 4, 1, DH)
    acc = data[7]
    run = logs[7]
    for piece in range(6, -1, -1):
        acc = acc + jnp.exp(run) * data[piece]
        run = run + logs[piece]
    f2s[...] = acc.reshape(32, DH).astype(BF16)
    f2r[z] = f2s[...]
    to_ring(send(1, lambda j: f2s, f2r.at[z]))

    sub = iota((1, 8, DH), 1).astype(F32)
    wide = jnp.concatenate(
        [jnp.broadcast_to(idr[:, 2 + r : 3 + r, :], (PLANE, 8, DH)) + sub for r in range(NR)], axis=1
    ).reshape(PLANE * 32, DH)
    lanes = iota((1, DH), 1).astype(F32)
    oh[:, 0:DH] = jnp.where(wide == lanes, 1.0, 0.0).astype(BF16)
    oh[:, DH : 2 * DH] = jnp.where(wide == lanes + float(DH), 1.0, 0.0).astype(BF16)

    wait_all(g1r.at[pl.ds(0, PLANE - 1)], recv_sems, 3)
    added = mm(oh[...], g1r[...].reshape(PLANE * 32, DH), 0, 0)
    g2s[...] = added.astype(BF16).reshape(RING, 32, DH)
    g2r[z] = g2s[z]
    to_ring(send(4, lambda j: g2s.at[j], g2r.at[z]))

    wait_all(f2r.at[pl.ds(0, RING - 1)], recv_sems, 1)
    picked = mm(oh[...], f2r[...].reshape(RING * 32, DH), 1, 0)
    f3s[...] = picked.astype(BF16).reshape(PLANE, 32, DH)
    f3r[me] = f3s[me]
    to_plane(send(2, lambda j: f3s.at[j], f3r.at[me]))

    after = jnp.zeros((8, DH), F32)
    for piece in range(8):
        after = after + jnp.where(piece > a, idr[piece * 4 + quad], 0.0)
    lane8 = iota((PIECE, 8), 1)
    pfac[:, 0:8] = jnp.exp(suf + jnp.where(lane8 == 0, after[0:1, 0:1], after[1:2, 0:1]))

    wait_all(g2r.at[pl.ds(0, RING - 1)], recv_sems, 4)
    g3s[...] = jnp.sum(g2r[...].astype(F32), axis=0).reshape(4, 8, DH)
    g3r[me] = g3s[quad]
    to_plane(send(5, lambda j: g3s.at[lax.rem(j, 4)], g3r.at[me]))

    inner(3)

    wait_all(g3r.at[pl.ds(0, PLANE - 1)], recv_sems, 5)
    gfin[...] = g3r[...].reshape(H * DH, DH)

    wait_all(f3r.at[pl.ds(0, PLANE - 1)], recv_sems, 2)
    got = f3r[...].astype(F32)
    for r in range(NR):
        starts[r] = got[:, r * 8 : (r + 1) * 8, :].reshape(2 * DH, DH).astype(BF16)

    wait_all(f1s.at[pl.ds(0, PLANE - 1)], send_sems, 0)
    wait_all(f2r.at[pl.ds(0, RING - 1)], send_sems, 1)
    wait_all(f3s.at[pl.ds(0, PLANE - 1)], send_sems, 2)
    wait_all(g1s.at[pl.ds(0, PLANE - 1)], send_sems, 3)
    wait_all(g2s.at[pl.ds(0, RING - 1)], send_sems, 4)
    wait_all(g3r.at[pl.ds(0, PLANE - 1)], send_sems, 5)
    wait_all(idr.at[pl.ds(0, PLANE - 1)], send_sems, 6)


def exchange(*args):
    hbm = pl.BlockSpec(memory_space=pltpu.HBM)
    vmem = pl.BlockSpec(memory_space=pltpu.VMEM)
    shapes = (
        ((1, PIECE, H * DH), BF16),
        ((1, PIECE, H * DH), BF16),
        ((NR, RMAX, H * DH), BF16),
        ((NR, RMAX, H * DH), BF16),
        ((NR, RMAX, H * DH), F32),
        ((NR, RMAX, H * DH), F32),
        ((NR, RMAX, H * DH), BF16),
        ((NR, RMAX, H * DH), BF16),
        ((NR, H * DH, DH), BF16),
        ((H * DH, DH), F32),
        ((CH, DH), F32),
        ((PIECE, DH), F32),
    )
    return pl.pallas_call(
        exchange_kernel,
        out_shape=tuple(pltpu.VMEM(s, t) for s, t in shapes),
        in_specs=[hbm] * 12,
        out_specs=(vmem,) * 12,
        scratch_shapes=[
            pltpu.SMEM((NR,), jnp.int32),
            pltpu.SMEM((1, NR), jnp.int32),
            pltpu.SMEM((NR,), jnp.int32),
            pltpu.VMEM((1, H, PIECE), F32),
            pltpu.VMEM((NR, RMAX, H * DH), BF16),
            pltpu.VMEM((NR, RMAX, H * DH), BF16),
            pltpu.VMEM((NR, H, RMAX), F32),
            pltpu.VMEM((NR, RMAX), jnp.int32),
            pltpu.VMEM((NR * 4, CH), F32),
            pltpu.VMEM((8, DH), F32),
            pltpu.VMEM((NR, H, DH, DH), BF16),
            pltpu.VMEM((PLANE, 8, DH), F32),
            pltpu.VMEM((PLANE, 8, DH), F32),
            pltpu.VMEM((8, DH), F32),
            pltpu.VMEM((PLANE, 8, DH), F32),
            pltpu.VMEM((32, DH), BF16),
            pltpu.VMEM((RING, 32, DH), BF16),
            pltpu.VMEM((PLANE, 32, DH), BF16),
            pltpu.VMEM((PLANE, 32, DH), BF16),
            pltpu.VMEM((PLANE, 32, DH), BF16),
            pltpu.VMEM((PLANE, 32, DH), BF16),
            pltpu.VMEM((RING, 32, DH), BF16),
            pltpu.VMEM((RING, 32, DH), BF16),
            pltpu.VMEM((4, 8, DH), F32),
            pltpu.VMEM((PLANE, 8, DH), F32),
            pltpu.VMEM((PLANE * 32, 2 * DH), BF16),
            pltpu.SemaphoreType.DMA((12,)),
            pltpu.SemaphoreType.DMA((7,)),
            pltpu.SemaphoreType.DMA((7,)),
        ],
        compiler_params=pltpu.CompilerParams(
            collective_id=0, has_side_effects=True, vmem_limit_bytes=32 << 20
        ),
        name="exchange",
    )(*args)


def finish_kernel(
    pk, pv, q, go, pout, pdq, dk, dv, starts, gfin, cols_ref, pfac,
    out_hbm, dq_hbm, dk_hbm, dv_hbm, pdk_hbm, pdv_hbm, out, dq, pdk, pdv, sems,
):
    early = [
        pltpu.make_async_copy(dk, dk_hbm, sems.at[0]),
        pltpu.make_async_copy(dv, dv_hbm, sems.at[1]),
    ]
    for c in early:
        c.start()
    cols = cols_ref[...]
    for r in range(NR):
        for h in range(H):
            hs = HEADS[h]
            state = starts[r, hs, :]
            span = None
            for c, t in enumerate(TOKENS):
                e = col(cols, r, 4 + 2 * c + h)
                if c == 1:
                    e = e * span
                span = e[CH - 1 : CH]
                o = pout[r, t, hs] + e * mm(q[r, t, hs], state, 1, 0)
                out[r, t, hs] = (o * col(cols, r, 12 + c)).astype(BF16)
                dq[r, t, hs] = (pdq[r, t, hs] + e * mm(go[r, t, hs], state, 1, 1)).astype(BF16)
        for i, (s, d) in enumerate(((out, out_hbm), (dq, dq_hbm))):
            c = pltpu.make_async_copy(s.at[r], d.at[r], sems.at[2 + 2 * r + i])
            c.start()
            early.append(c)
    for h in range(H):
        hs = HEADS[h]
        factor = pfac[:, h : h + 1]
        hi, lo = split(gfin[hs, :])
        vh, kh = pv[0, :, hs], pk[0, :, hs]
        pdk[0, :, hs] = (factor * (mm(vh, hi, 1, 1) + mm(vh, lo, 1, 1))).astype(BF16)
        pdv[0, :, hs] = (factor * (mm(kh, hi, 1, 0) + mm(kh, lo, 1, 0))).astype(BF16)
    for i, (s, d) in enumerate(((pdk, pdk_hbm), (pdv, pdv_hbm))):
        c = pltpu.make_async_copy(s, d, sems.at[10 + i])
        c.start()
        early.append(c)
    for c in early:
        c.wait()


def finish(*parts):
    vmem = pl.BlockSpec(memory_space=pltpu.VMEM)
    hbm = pl.BlockSpec(memory_space=pltpu.HBM)
    big = jax.ShapeDtypeStruct((NR, RMAX, H * DH), BF16)
    small = jax.ShapeDtypeStruct((1, PIECE, H * DH), BF16)
    return pl.pallas_call(
        finish_kernel,
        out_shape=(big,) * 4 + (small,) * 2,
        in_specs=[vmem] * 12,
        out_specs=(hbm,) * 6,
        scratch_shapes=[
            pltpu.VMEM((NR, RMAX, H * DH), BF16),
            pltpu.VMEM((NR, RMAX, H * DH), BF16),
            pltpu.VMEM((1, PIECE, H * DH), BF16),
            pltpu.VMEM((1, PIECE, H * DH), BF16),
            pltpu.SemaphoreType.DMA((12,)),
        ],
        compiler_params=pltpu.CompilerParams(vmem_limit_bytes=24 << 20),
        name="finish",
    )(*parts)


def shards(pk, pv, pg, q, k, v, rg, cot, gid, lens, mask, adv):
    parts = exchange(*[pltpu.with_memory_space_constraint(x, pltpu.HBM) for x in (gid, lens, adv, pk, pv, pg, q, k, v, cot, rg, mask)])
    return finish(*parts)


def solution(mesh):
    both = ("prompt", "resp")
    pieces = P("resp", "prompt", None)
    slots = P(both, None, None)
    return jax.shard_map(
        shards,
        mesh=mesh,
        in_specs=(
            pieces,
            pieces,
            P("resp", None, "prompt"),
            slots,
            slots,
            slots,
            slots,
            slots,
            P(both),
            P(both, None),
            P(both, None),
            P(both),
        ),
        out_specs=(slots, slots, slots, slots, pieces, pieces),
        check_vma=False,
    )
```

```python
import jax
import jax.numpy as jnp
from jax import lax
from jax.experimental import pallas as pl
from jax.experimental.pallas import tpu as pltpu
from jax.sharding import PartitionSpec as P

H = 2
DH = 128
RMAX = 512
NR = 4
PIECE = 256
PLANE = 32
RING = 8
CH = 256
HI = lax.Precision.HIGHEST
MESH = pl.DeviceIdType.MESH
F32 = jnp.float32
BF16 = jnp.bfloat16
HEADS = [slice(h * DH, (h + 1) * DH) for h in range(H)]
TOKENS = [slice(c * CH, (c + 1) * CH) for c in range(RMAX // CH)]


def mm(x, y, cx, cy, **kw):
    return lax.dot_general(x, y, (((cx,), (cy,)), ((), ())), preferred_element_type=F32, **kw)


def split(x):
    hi = x.astype(BF16)
    return hi, (x - hi.astype(F32)).astype(BF16)


def iota(shape, axis):
    return lax.broadcasted_iota(jnp.int32, shape, axis)


def col(cols, r, item):
    return cols[:, r * 16 + item : r * 16 + item + 1]


def exchange_kernel(
    gid_hbm, lens_hbm, adv_hbm, pk_hbm, pv_hbm, pg_hbm, q_hbm, k_hbm, v_hbm, cot_hbm, rg_hbm, mask_hbm,
    pk, pv, q, go, pout, pdq, dk, dv, starts, gfin, cols_out, pfac,
    gid, lens, adv, pg, k, v, rg, mask, crows, back,
    f1s, f1r, ids, idr, f2s, f2r, f3s, f3r, g1s, g1r, g2s, g2r, g3s, g3r, oh, oht,
    in_sems, send_sems, recv_sems,
):
    a = lax.axis_index("prompt")
    b = lax.axis_index("resp")
    quad = lax.div(b, 16) * 2 + lax.rem(b, 2)
    z = lax.rem(lax.div(b, 2), RING)
    me = a * 4 + quad
    near, core = lax.div(b, 16), lax.rem(b, 2)
    columns = {
        (fx, dy): lax.rem(lax.div(a, 4) + fx, 2) * 4 + lax.rem(lax.rem(a, 4) + dy, 4)
        for fx in range(2)
        for dy in range(4)
    }
    quads, homes = {}, {}
    for fh in range(2):
        for fc in range(2):
            hi, lo = lax.rem(near + fh, 2), lax.rem(core + fc, 2)
            quads[fh, fc] = hi * 2 + lo
            homes[fh, fc] = hi * 16 + z * 2 + lo
    order = sorted(
        ((fx, dy, fh, fc) for fx in range(2) for dy in range(4) for fh in range(2) for fc in range(2)),
        key=lambda p: -((1 if p[0] else 2 * p[2]) + (0, 1, 2, 1)[p[1]]) * 2 - p[3],
    )
    order.remove((0, 0, 0, 0))
    corner = lax.div(b, 16) * 16 + lax.rem(b, 2)
    rings = [lax.rem(z + d, RING) for d in (4, 3, 5, 2, 6, 1, 7)]

    loads = [
        pltpu.make_async_copy(s, d, in_sems.at[i])
        for i, (s, d) in enumerate(
            (
                (pg_hbm, pg), (rg_hbm, rg), (lens_hbm, lens), (adv_hbm, adv), (mask_hbm, mask), (gid_hbm, gid),
                (pk_hbm, pk), (pv_hbm, pv), (cot_hbm, go), (q_hbm, q), (k_hbm, k), (v_hbm, v),
            )
        )
    ]
    for c in loads:
        c.start()

    def to_plane(fn):
        for fx, dy, fh, fc in order:
            aa = columns[fx, dy]
            fn(aa * 4 + quads[fh, fc], (aa, homes[fh, fc]))

    def to_ring(fn):
        for zz in rings:
            fn(zz, (a, corner + zz * 2))

    barrier = pltpu.get_barrier_semaphore()

    def greet(_, dev):
        pl.semaphore_signal(barrier, inc=1, device_id=dev, device_id_type=MESH)

    to_plane(greet)
    to_ring(greet)

    def send(stage, src_of, dst):
        def one(j, dev):
            pltpu.make_async_remote_copy(
                src_ref=src_of(j),
                dst_ref=dst,
                send_sem=send_sems.at[stage],
                recv_sem=recv_sems.at[stage],
                device_id=dev,
                device_id_type=MESH,
            ).start()

        return one

    def wait_all(ref, sems, stage):
        pltpu.make_async_copy(ref, ref, sems.at[stage]).wait()

    for c in loads[:5]:
        c.wait()
    upper = (iota((CH, CH), 0) <= iota((CH, CH), 1)).astype(F32)
    lane = iota((1, CH), 1)
    grows = jnp.concatenate([rg[r, :, t] for r in range(NR) for t in TOKENS] + [pg[0]], axis=0)
    cums = mm(grows, upper, 1, 0, precision=HI)
    crows[...] = cums[: NR * 4]
    exps = jnp.exp(cums)
    tots = cums[:, CH - 1 : CH]
    falls = jnp.exp(tots - cums)
    rows = []
    for r in range(NR):
        rows += [cums[4 * r : 4 * r + 4], exps[4 * r : 4 * r + 4]]
        opens = [jnp.where(lane + c * CH < lens[0, r], 1.0, 0.0) for c in range(len(TOKENS))]
        for on, t in zip(opens, TOKENS):
            rows.append(on * mask[r : r + 1, t].astype(F32) * (adv[r].astype(F32) * (1.0 / 1024.0)))
        rows += [falls[4 * r : 4 * r + 2]] + opens + [jnp.zeros((2, CH), F32)]
    rows += [falls[NR * 4 : NR * 4 + 2], jnp.zeros((62, CH), F32)]
    cols = jnp.concatenate(rows, axis=0).T
    cols_out[...] = cols

    for c in loads[5:8]:
        c.wait()
    for h in range(H):
        hi, lo = split(cols[:, 64 + h : 65 + h] * pv[0, :, HEADS[h]].astype(F32))
        kh = pk[0, :, HEADS[h]]
        state = mm(kh, hi, 0, 0) + mm(kh, lo, 0, 0)
        f1s[h * 16 : (h + 1) * 16] = state.reshape(16, 8, DH).astype(BF16)
    lane = iota((1, DH), 1)
    meta = jnp.zeros((1, DH), F32)
    for h in range(H):
        meta = jnp.where(lane == h, tots[NR * 4 + h : NR * 4 + h + 1], meta)
    for r in range(NR):
        g = gid[r]
        slot = ((g >> 1) & 7) * 4 + (g >> 4) * 2 + (g & 1)
        meta = jnp.where(lane == 2 + r, (slot * 8).astype(F32), meta)
    ids[...] = meta
    f1r[me] = f1s[me]
    idr[me] = meta

    for c in loads[8:10]:
        c.wait()
    for pair in range(NR // 2):
        for h in range(H):
            found = []
            for r in (2 * pair, 2 * pair + 1):
                parts = []
                for c, t in enumerate(TOKENS):
                    grad_out = (go[r, t, HEADS[h]].astype(F32) * col(cols, r, 8 + c)).astype(BF16)
                    go[r, t, HEADS[h]] = grad_out
                    scaled = (grad_out.astype(F32) * col(cols, r, 4 + 2 * c + h)).astype(BF16)
                    parts.append(mm(q[r, t, HEADS[h]], scaled, 0, 0))
                back[r, h] = parts[1].astype(BF16)
                fall = jnp.exp(tots[4 * r + h : 4 * r + h + 1])
                found.append((parts[0] + fall * parts[1]).reshape(16, 8, DH))
            g1s[h * 16 : (h + 1) * 16, pair * 16 : (pair + 1) * 16, :] = jnp.concatenate(
                found, axis=1
            ).astype(BF16)
    g1r[me] = g1s[me]

    pl.semaphore_wait(barrier, PLANE - 1 + RING - 1)
    to_plane(send(6, lambda j: ids, idr.at[me]))
    to_plane(send(0, lambda j: f1s.at[j], f1r.at[me]))
    to_plane(send(3, lambda j: g1s.at[j], g1r.at[me]))

    loads[10].wait()
    loads[11].wait()
    causal = iota((CH, CH), 0) >= iota((CH, CH), 1)

    def inner(r):
        for h in range(H):
            hs = HEADS[h]
            bk = back[r, h]
            step = None
            for c, t in enumerate(TOKENS):
                qc, kc, vc, gc = q[r, t, hs], k[r, t, hs], v[r, t, hs], go[r, t, hs]
                i = 4 * r + 2 * c + h
                decay = jnp.exp(jnp.where(causal, col(cols, r, 2 * c + h) - crows[i : i + 1, :], -1e30))
                mix = (mm(qc, kc, 1, 1) * decay).astype(BF16)
                gs = (mm(gc, vc, 1, 1) * decay).astype(BF16)
                out = mm(mix, vc, 1, 0)
                dq = mm(gs, kc, 1, 0)
                dkc = mm(gs, qc, 0, 0)
                dvc = mm(mix, gc, 0, 0)
                if c == 0:
                    f = col(cols, r, 10 + h)
                    dkc = dkc + f * mm(vc, bk, 1, 1)
                    dvc = dvc + f * mm(kc, bk, 1, 0)
                    step = mm(kc, (f * vc.astype(F32)).astype(BF16), 0, 0).astype(BF16)
                else:
                    e = col(cols, r, 4 + 2 * c + h)
                    out = out + e * mm(qc, step, 1, 0)
                    dq = dq + e * mm(gc, step, 1, 1)
                pout[r, t, hs] = out
                pdq[r, t, hs] = dq
                dk[r, t, hs] = dkc.astype(BF16)
                dv[r, t, hs] = dvc.astype(BF16)

    inner(0)
    inner(1)

    wait_all(idr.at[pl.ds(0, PLANE - 1)], recv_sems, 6)
    sub = iota((1, 8, DH), 1).astype(F32)
    wide = jnp.concatenate(
        [jnp.broadcast_to(idr[:, :, 2 + r : 3 + r], (PLANE, 8, DH)) + sub for r in range(NR)], axis=1
    ).reshape(PLANE * 32, DH)
    lanes = iota((1, DH), 1).astype(F32)
    picks = [jnp.where(wide == lanes + float(i * DH), 1.0, 0.0).astype(BF16) for i in range(2)]
    for i in range(2):
        oh[:, i * DH : (i + 1) * DH] = picks[i]
        oht[i * DH : (i + 1) * DH, :] = picks[i].T
    logs = idr[...].reshape(8, 4, 1, DH)
    run = logs[7]
    keeps = []
    for piece in range(6, -1, -1):
        keep = jnp.exp(run)
        keeps.append(jnp.where(a >= 4, keep[:, :, 1:2], keep[:, :, 0:1]))
        run = run + logs[piece]

    wait_all(f1r.at[pl.ds(0, PLANE - 1)], recv_sems, 0)
    data = f1r[...].astype(F32).reshape(8, 4, 8, DH)
    acc = data[7]
    for piece in range(6, -1, -1):
        acc = acc + keeps[6 - piece] * data[piece]
    f2s[...] = acc.reshape(32, DH).astype(BF16)
    f2r[z] = f2s[...]
    to_ring(send(1, lambda j: f2s, f2r.at[z]))

    inner(2)

    wait_all(g1r.at[pl.ds(0, PLANE - 1)], recv_sems, 3)
    added = mm(oht[...], g1r[...].reshape(PLANE * 32, DH), 1, 0)
    g2s[...] = added.astype(BF16).reshape(RING, 32, DH)
    g2r[z] = g2s[z]
    to_ring(send(4, lambda j: g2s.at[j], g2r.at[z]))

    wait_all(f2r.at[pl.ds(0, RING - 1)], recv_sems, 1)
    picked = mm(oh[...], f2r[...].reshape(RING * 32, DH), 1, 0)
    f3s[...] = picked.astype(BF16).reshape(PLANE, 32, DH)
    f3r[me] = f3s[me]
    to_plane(send(2, lambda j: f3s.at[j], f3r.at[me]))

    after = jnp.zeros((1, DH), F32)
    for piece in range(8):
        after = after + jnp.where(piece > a, idr[piece * 4 + quad], 0.0)
    pfac[...] = jnp.exp(after)

    wait_all(g2r.at[pl.ds(0, RING - 1)], recv_sems, 4)
    g3s[...] = jnp.sum(g2r[...].astype(F32), axis=0).reshape(4, 8, DH).astype(BF16)
    g3r[me] = g3s[quad]
    to_plane(send(5, lambda j: g3s.at[lax.rem(j, 4)], g3r.at[me]))

    inner(3)

    wait_all(g3r.at[pl.ds(0, PLANE - 1)], recv_sems, 5)
    gfin[...] = g3r[...].astype(F32).reshape(H * DH, DH).astype(BF16)

    wait_all(f3r.at[pl.ds(0, PLANE - 1)], recv_sems, 2)
    got = f3r[...].astype(F32)
    for r in range(NR):
        starts[r] = got[:, r * 8 : (r + 1) * 8, :].reshape(2 * DH, DH).astype(BF16)

    wait_all(f1s.at[pl.ds(0, PLANE - 1)], send_sems, 0)
    wait_all(f2r.at[pl.ds(0, RING - 1)], send_sems, 1)
    wait_all(f3s.at[pl.ds(0, PLANE - 1)], send_sems, 2)
    wait_all(g1s.at[pl.ds(0, PLANE - 1)], send_sems, 3)
    wait_all(g2s.at[pl.ds(0, RING - 1)], send_sems, 4)
    wait_all(g3r.at[pl.ds(0, PLANE - 1)], send_sems, 5)
    wait_all(idr.at[pl.ds(0, PLANE - 1)], send_sems, 6)


def exchange(*args):
    hbm = pl.BlockSpec(memory_space=pltpu.HBM)
    vmem = pl.BlockSpec(memory_space=pltpu.VMEM)
    shapes = (
        ((1, PIECE, H * DH), BF16),
        ((1, PIECE, H * DH), BF16),
        ((NR, RMAX, H * DH), BF16),
        ((NR, RMAX, H * DH), BF16),
        ((NR, RMAX, H * DH), F32),
        ((NR, RMAX, H * DH), F32),
        ((NR, RMAX, H * DH), BF16),
        ((NR, RMAX, H * DH), BF16),
        ((NR, H * DH, DH), BF16),
        ((H * DH, DH), BF16),
        ((CH, DH), F32),
        ((1, DH), F32),
    )
    return pl.pallas_call(
        exchange_kernel,
        out_shape=tuple(pltpu.VMEM(s, t) for s, t in shapes),
        in_specs=[hbm] * 12,
        out_specs=(vmem,) * 12,
        scratch_shapes=[
            pltpu.SMEM((NR,), jnp.int32),
            pltpu.SMEM((1, NR), jnp.int32),
            pltpu.SMEM((NR,), jnp.int32),
            pltpu.VMEM((1, H, PIECE), F32),
            pltpu.VMEM((NR, RMAX, H * DH), BF16),
            pltpu.VMEM((NR, RMAX, H * DH), BF16),
            pltpu.VMEM((NR, H, RMAX), F32),
            pltpu.VMEM((NR, RMAX), jnp.int32),
            pltpu.VMEM((NR * 4, CH), F32),
            pltpu.VMEM((NR, H, DH, DH), BF16),
            pltpu.VMEM((PLANE, 8, DH), BF16),
            pltpu.VMEM((PLANE, 8, DH), BF16),
            pltpu.VMEM((1, DH), F32),
            pltpu.VMEM((PLANE, 1, DH), F32),
            pltpu.VMEM((32, DH), BF16),
            pltpu.VMEM((RING, 32, DH), BF16),
            pltpu.VMEM((PLANE, 32, DH), BF16),
            pltpu.VMEM((PLANE, 32, DH), BF16),
            pltpu.VMEM((PLANE, 32, DH), BF16),
            pltpu.VMEM((PLANE, 32, DH), BF16),
            pltpu.VMEM((RING, 32, DH), BF16),
            pltpu.VMEM((RING, 32, DH), BF16),
            pltpu.VMEM((4, 8, DH), BF16),
            pltpu.VMEM((PLANE, 8, DH), BF16),
            pltpu.VMEM((PLANE * 32, 2 * DH), BF16),
            pltpu.VMEM((2 * DH, PLANE * 32), BF16),
            pltpu.SemaphoreType.DMA((12,)),
            pltpu.SemaphoreType.DMA((7,)),
            pltpu.SemaphoreType.DMA((7,)),
        ],
        compiler_params=pltpu.CompilerParams(
            collective_id=0, has_side_effects=True, vmem_limit_bytes=32 << 20
        ),
        name="exchange",
    )(*args)


def finish_kernel(
    pk, pv, q, go, pout, pdq, dk, dv, starts, gfin, cols_ref, pfac,
    out_hbm, dq_hbm, dk_hbm, dv_hbm, pdk_hbm, pdv_hbm, out, dq, pdk, pdv, sems,
):
    early = [
        pltpu.make_async_copy(dk, dk_hbm, sems.at[0]),
        pltpu.make_async_copy(dv, dv_hbm, sems.at[1]),
    ]
    for c in early:
        c.start()
    cols = cols_ref[...]
    for r in range(NR):
        for h in range(H):
            hs = HEADS[h]
            state = starts[r, hs, :]
            span = None
            for c, t in enumerate(TOKENS):
                e = col(cols, r, 4 + 2 * c + h)
                if c == 1:
                    e = e * span
                span = e[CH - 1 : CH]
                o = pout[r, t, hs] + e * mm(q[r, t, hs], state, 1, 0)
                out[r, t, hs] = (o * col(cols, r, 12 + c)).astype(BF16)
                dq[r, t, hs] = (pdq[r, t, hs] + e * mm(go[r, t, hs], state, 1, 1)).astype(BF16)
        for i, (s, d) in enumerate(((out, out_hbm), (dq, dq_hbm))):
            c = pltpu.make_async_copy(s.at[r], d.at[r], sems.at[2 + 2 * r + i])
            c.start()
            early.append(c)
    for h in range(H):
        hs = HEADS[h]
        factor = cols[:, 64 + h : 65 + h] * pfac[:, h : h + 1]
        g = gfin[hs, :]
        pdk[0, :, hs] = (factor * mm(pv[0, :, hs], g, 1, 1)).astype(BF16)
        pdv[0, :, hs] = (factor * mm(pk[0, :, hs], g, 1, 0)).astype(BF16)
    for i, (s, d) in enumerate(((pdk, pdk_hbm), (pdv, pdv_hbm))):
        c = pltpu.make_async_copy(s, d, sems.at[10 + i])
        c.start()
        early.append(c)
    for c in early:
        c.wait()


def finish(*parts):
    vmem = pl.BlockSpec(memory_space=pltpu.VMEM)
    hbm = pl.BlockSpec(memory_space=pltpu.HBM)
    big = jax.ShapeDtypeStruct((NR, RMAX, H * DH), BF16)
    small = jax.ShapeDtypeStruct((1, PIECE, H * DH), BF16)
    return pl.pallas_call(
        finish_kernel,
        out_shape=(big,) * 4 + (small,) * 2,
        in_specs=[vmem] * 12,
        out_specs=(hbm,) * 6,
        scratch_shapes=[
            pltpu.VMEM((NR, RMAX, H * DH), BF16),
            pltpu.VMEM((NR, RMAX, H * DH), BF16),
            pltpu.VMEM((1, PIECE, H * DH), BF16),
            pltpu.VMEM((1, PIECE, H * DH), BF16),
            pltpu.SemaphoreType.DMA((12,)),
        ],
        compiler_params=pltpu.CompilerParams(vmem_limit_bytes=24 << 20),
        name="finish",
    )(*parts)


def shards(pk, pv, pg, q, k, v, rg, cot, gid, lens, mask, adv):
    parts = exchange(*[pltpu.with_memory_space_constraint(x, pltpu.HBM) for x in (gid, lens, adv, pk, pv, pg, q, k, v, cot, rg, mask)])
    return finish(*parts)


def solution(mesh):
    both = ("prompt", "resp")
    pieces = P("resp", "prompt", None)
    slots = P(both, None, None)
    return jax.shard_map(
        shards,
        mesh=mesh,
        in_specs=(
            pieces,
            pieces,
            P("resp", None, "prompt"),
            slots,
            slots,
            slots,
            slots,
            slots,
            P(both),
            P(both, None),
            P(both, None),
            P(both),
        ),
        out_specs=(slots, slots, slots, slots, pieces, pieces),
        check_vma=False,
    )
```

```python
import jax
import jax.numpy as jnp
from jax import lax
from jax.experimental import pallas as pl
from jax.experimental.pallas import tpu as pltpu
from jax.sharding import PartitionSpec as P

H = 2
DH = 128
RMAX = 512
NR = 4
PIECE = 256
PLANE = 32
RING = 8
CH = 256
HI = lax.Precision.HIGHEST
MESH = pl.DeviceIdType.MESH
F32 = jnp.float32
BF16 = jnp.bfloat16
HEADS = [slice(h * DH, (h + 1) * DH) for h in range(H)]
TOKENS = [slice(c * CH, (c + 1) * CH) for c in range(RMAX // CH)]


def mm(x, y, cx, cy, **kw):
    return lax.dot_general(x, y, (((cx,), (cy,)), ((), ())), preferred_element_type=F32, **kw)


def split(x):
    hi = x.astype(BF16)
    return hi, (x - hi.astype(F32)).astype(BF16)


def iota(shape, axis):
    return lax.broadcasted_iota(jnp.int32, shape, axis)


def col(cols, r, item):
    return cols[:, r * 16 + item : r * 16 + item + 1]


def exchange_kernel(
    gid_hbm, lens_hbm, adv_hbm, pk_hbm, pv_hbm, pg_hbm, q_hbm, k_hbm, v_hbm, cot_hbm, rg_hbm, mask_hbm,
    pk, pv, q, go, pout, pdq, dk, dv, starts, gfin, cols_out, pfac,
    gid, lens, adv, pg, k, v, rg, mask, crows, back,
    f1s, f1r, ids, idr, f2s, f2r, f3s, f3r, g1s, g1r, g2s, g2r, g3s, g3r, oh, oht,
    in_sems, send_sems, recv_sems,
):
    a = lax.axis_index("prompt")
    b = lax.axis_index("resp")
    quad = lax.div(b, 16) * 2 + lax.rem(b, 2)
    z = lax.rem(lax.div(b, 2), RING)
    me = a * 4 + quad
    near, core = lax.div(b, 16), lax.rem(b, 2)
    columns = {
        (fx, dy): lax.rem(lax.div(a, 4) + fx, 2) * 4 + lax.rem(lax.rem(a, 4) + dy, 4)
        for fx in range(2)
        for dy in range(4)
    }
    quads, homes = {}, {}
    for fh in range(2):
        for fc in range(2):
            hi, lo = lax.rem(near + fh, 2), lax.rem(core + fc, 2)
            quads[fh, fc] = hi * 2 + lo
            homes[fh, fc] = hi * 16 + z * 2 + lo
    order = sorted(
        ((fx, dy, fh, fc) for fx in range(2) for dy in range(4) for fh in range(2) for fc in range(2)),
        key=lambda p: -((1 if p[0] else 2 * p[2]) + (0, 1, 2, 1)[p[1]]) * 2 - p[3],
    )
    order.remove((0, 0, 0, 0))
    corner = lax.div(b, 16) * 16 + lax.rem(b, 2)
    rings = [lax.rem(z + d, RING) for d in (4, 3, 5, 2, 6, 1, 7)]

    loads = [
        pltpu.make_async_copy(s, d, in_sems.at[i])
        for i, (s, d) in enumerate(
            (
                (pg_hbm, pg), (rg_hbm, rg), (lens_hbm, lens), (adv_hbm, adv), (mask_hbm, mask), (gid_hbm, gid),
                (pk_hbm, pk), (pv_hbm, pv), (cot_hbm, go), (q_hbm, q), (k_hbm, k), (v_hbm, v),
            )
        )
    ]
    for c in loads[:8]:
        c.start()

    def to_plane(fn):
        for fx, dy, fh, fc in order:
            aa = columns[fx, dy]
            fn(aa * 4 + quads[fh, fc], (aa, homes[fh, fc]))

    def to_ring(fn):
        for zz in rings:
            fn(zz, (a, corner + zz * 2))

    barrier = pltpu.get_barrier_semaphore()

    def greet(_, dev):
        pl.semaphore_signal(barrier, inc=1, device_id=dev, device_id_type=MESH)

    to_plane(greet)
    to_ring(greet)
    for c in loads[8:]:
        c.start()

    def send(stage, src_of, dst):
        def one(j, dev):
            pltpu.make_async_remote_copy(
                src_ref=src_of(j),
                dst_ref=dst,
                send_sem=send_sems.at[stage],
                recv_sem=recv_sems.at[stage],
                device_id=dev,
                device_id_type=MESH,
            ).start()

        return one

    def wait_all(ref, sems, stage):
        pltpu.make_async_copy(ref, ref, sems.at[stage]).wait()

    for c in loads[:5]:
        c.wait()
    upper = jnp.where(iota((CH, CH), 0) <= iota((CH, CH), 1), 1.0, 0.0).astype(BF16)
    lane = iota((1, CH), 1)
    grows = jnp.concatenate([rg[r, :, t] for r in range(NR) for t in TOKENS] + [pg[0]], axis=0)
    high, rest = grows.astype(BF16), grows
    rest = rest - high.astype(F32)
    middle, low = split(rest)
    cums = mm(high, upper, 1, 0) + (mm(middle, upper, 1, 0) + mm(low, upper, 1, 0))
    crows[...] = cums[: NR * 4]
    exps = jnp.exp(cums)
    tots = cums[:, CH - 1 : CH]
    falls = jnp.exp(tots - cums)
    rows = []
    for r in range(NR):
        rows += [cums[4 * r : 4 * r + 4], exps[4 * r : 4 * r + 4]]
        opens = [jnp.where(lane + c * CH < lens[0, r], 1.0, 0.0) for c in range(len(TOKENS))]
        for on, t in zip(opens, TOKENS):
            rows.append(on * mask[r : r + 1, t].astype(F32) * (adv[r].astype(F32) * (1.0 / 1024.0)))
        fall = jnp.exp(tots[4 * r : 4 * r + 2])
        rows += [
            falls[4 * r : 4 * r + 2],
            exps[4 * r : 4 * r + 2] * opens[0],
            exps[4 * r + 2 : 4 * r + 4] * fall * opens[1],
        ]
    rows += [falls[NR * 4 : NR * 4 + 2], jnp.zeros((62, CH), F32)]
    cols = jnp.concatenate(rows, axis=0).T
    cols_out[...] = cols

    for c in loads[5:8]:
        c.wait()
    for h in range(H):
        hi, lo = split(cols[:, 64 + h : 65 + h] * pv[0, :, HEADS[h]].astype(F32))
        kh = pk[0, :, HEADS[h]]
        state = mm(kh, hi, 0, 0) + mm(kh, lo, 0, 0)
        f1s[h * 16 : (h + 1) * 16] = state.reshape(16, 8, DH).astype(BF16)
    lane = iota((1, DH), 1)
    meta = jnp.zeros((1, DH), F32)
    for h in range(H):
        meta = jnp.where(lane == h, tots[NR * 4 + h : NR * 4 + h + 1], meta)
    for r in range(NR):
        g = gid[r]
        slot = ((g >> 1) & 7) * 4 + (g >> 4) * 2 + (g & 1)
        meta = jnp.where(lane == 2 + r, (slot * 8).astype(F32), meta)
    ids[...] = meta
    f1r[me] = f1s[me]
    idr[me] = meta

    for c in loads[8:10]:
        c.wait()
    for pair in range(NR // 2):
        for h in range(H):
            found = []
            for r in (2 * pair, 2 * pair + 1):
                parts = []
                for c, t in enumerate(TOKENS):
                    grad_out = (go[r, t, HEADS[h]].astype(F32) * col(cols, r, 8 + c)).astype(BF16)
                    go[r, t, HEADS[h]] = grad_out
                    scaled = (grad_out.astype(F32) * col(cols, r, 4 + 2 * c + h)).astype(BF16)
                    parts.append(mm(q[r, t, HEADS[h]], scaled, 0, 0))
                back[r, h] = parts[1].astype(BF16)
                fall = jnp.exp(tots[4 * r + h : 4 * r + h + 1])
                found.append((parts[0] + fall * parts[1]).reshape(16, 8, DH))
            g1s[h * 16 : (h + 1) * 16, pair * 16 : (pair + 1) * 16, :] = jnp.concatenate(
                found, axis=1
            ).astype(BF16)
    g1r[me] = g1s[me]

    pl.semaphore_wait(barrier, PLANE - 1 + RING - 1)
    to_plane(send(6, lambda j: ids, idr.at[me]))
    to_plane(send(0, lambda j: f1s.at[j], f1r.at[me]))
    to_plane(send(3, lambda j: g1s.at[j], g1r.at[me]))

    loads[10].wait()
    loads[11].wait()
    causal = iota((CH, CH), 0) >= iota((CH, CH), 1)
    place = iota((CH, DH), 0)

    def inner(r):
        for h in range(H):
            hs = HEADS[h]
            bk = back[r, h]
            step = None
            for c, t in enumerate(TOKENS):
                qc, kc, vc, gc = q[r, t, hs], k[r, t, hs], v[r, t, hs], go[r, t, hs]
                i = 4 * r + 2 * c + h
                decay = jnp.exp(jnp.where(causal, col(cols, r, 2 * c + h) - crows[i : i + 1, :], -1e30))
                mix = (mm(qc, kc, 1, 1) * decay).astype(BF16)
                gs = (mm(gc, vc, 1, 1) * decay).astype(BF16)
                out = mm(mix, vc, 1, 0)
                dq = mm(gs, kc, 1, 0)
                dkc = mm(gs, qc, 0, 0)
                dvc = mm(mix, gc, 0, 0)
                if c == 0:
                    f = col(cols, r, 10 + h)
                    dkc = dkc + f * mm(vc, bk, 1, 1)
                    dvc = dvc + f * mm(kc, bk, 1, 0)
                    step = mm(kc, (f * vc.astype(F32)).astype(BF16), 0, 0).astype(BF16)
                else:
                    e = col(cols, r, 4 + 2 * c + h)
                    out = out + e * mm(qc, step, 1, 0)
                    dq = dq + e * mm(gc, step, 1, 1)
                pout[r, t, hs] = jnp.where(place + c * CH < lens[0, r], out, 0.0)
                pdq[r, t, hs] = dq
                dk[r, t, hs] = dkc.astype(BF16)
                dv[r, t, hs] = dvc.astype(BF16)

    inner(0)
    inner(1)

    wait_all(idr.at[pl.ds(0, PLANE - 1)], recv_sems, 6)
    sub = iota((1, 8, DH), 1).astype(F32)
    wide = jnp.concatenate(
        [jnp.broadcast_to(idr[:, :, 2 + r : 3 + r], (PLANE, 8, DH)) + sub for r in range(NR)], axis=1
    ).reshape(PLANE * 32, DH)
    lanes = iota((1, DH), 1).astype(F32)
    picks = [jnp.where(wide == lanes + float(i * DH), 1.0, 0.0).astype(BF16) for i in range(2)]
    for i in range(2):
        oh[:, i * DH : (i + 1) * DH] = picks[i]
        oht[i * DH : (i + 1) * DH, :] = picks[i].T
    logs = idr[...].reshape(8, 4, 1, DH)
    run = logs[7]
    keeps = []
    for piece in range(6, -1, -1):
        keep = jnp.exp(run)
        keeps.append(jnp.where(a >= 4, keep[:, :, 1:2], keep[:, :, 0:1]))
        run = run + logs[piece]

    wait_all(f1r.at[pl.ds(0, PLANE - 1)], recv_sems, 0)
    data = f1r[...].astype(F32).reshape(8, 4, 8, DH)
    acc = data[7]
    for piece in range(6, -1, -1):
        acc = acc + keeps[6 - piece] * data[piece]
    f2s[...] = acc.reshape(32, DH).astype(BF16)
    f2r[z] = f2s[...]
    to_ring(send(1, lambda j: f2s, f2r.at[z]))

    inner(2)

    wait_all(g1r.at[pl.ds(0, PLANE - 1)], recv_sems, 3)
    added = mm(oht[...], g1r[...].reshape(PLANE * 32, DH), 1, 0)
    g2s[...] = added.astype(BF16).reshape(RING, 32, DH)
    g2r[z] = g2s[z]
    to_ring(send(4, lambda j: g2s.at[j], g2r.at[z]))

    wait_all(f2r.at[pl.ds(0, RING - 1)], recv_sems, 1)
    picked = mm(oh[...], f2r[...].reshape(RING * 32, DH), 1, 0)
    f3s[...] = picked.astype(BF16).reshape(PLANE, 32, DH)
    f3r[me] = f3s[me]
    to_plane(send(2, lambda j: f3s.at[j], f3r.at[me]))

    after = jnp.zeros((1, DH), F32)
    for piece in range(8):
        after = after + jnp.where(piece > a, idr[piece * 4 + quad], 0.0)
    pfac[...] = jnp.exp(after)

    wait_all(g2r.at[pl.ds(0, RING - 1)], recv_sems, 4)
    g3s[...] = jnp.sum(g2r[...].astype(F32), axis=0).reshape(4, 8, DH).astype(BF16)
    g3r[me] = g3s[quad]
    to_plane(send(5, lambda j: g3s.at[lax.rem(j, 4)], g3r.at[me]))

    inner(3)

    wait_all(g3r.at[pl.ds(0, PLANE - 1)], recv_sems, 5)
    gfin[...] = g3r[...].astype(F32).reshape(H * DH, DH).astype(BF16)

    wait_all(f3r.at[pl.ds(0, PLANE - 1)], recv_sems, 2)
    got = f3r[...].astype(F32)
    for r in range(NR):
        starts[r] = got[:, r * 8 : (r + 1) * 8, :].reshape(2 * DH, DH).astype(BF16)

    wait_all(f1s.at[pl.ds(0, PLANE - 1)], send_sems, 0)
    wait_all(f2r.at[pl.ds(0, RING - 1)], send_sems, 1)
    wait_all(f3s.at[pl.ds(0, PLANE - 1)], send_sems, 2)
    wait_all(g1s.at[pl.ds(0, PLANE - 1)], send_sems, 3)
    wait_all(g2s.at[pl.ds(0, RING - 1)], send_sems, 4)
    wait_all(g3r.at[pl.ds(0, PLANE - 1)], send_sems, 5)
    wait_all(idr.at[pl.ds(0, PLANE - 1)], send_sems, 6)


def exchange(*args):
    hbm = pl.BlockSpec(memory_space=pltpu.HBM)
    vmem = pl.BlockSpec(memory_space=pltpu.VMEM)
    shapes = (
        ((1, PIECE, H * DH), BF16),
        ((1, PIECE, H * DH), BF16),
        ((NR, RMAX, H * DH), BF16),
        ((NR, RMAX, H * DH), BF16),
        ((NR, RMAX, H * DH), F32),
        ((NR, RMAX, H * DH), F32),
        ((NR, RMAX, H * DH), BF16),
        ((NR, RMAX, H * DH), BF16),
        ((NR, H * DH, DH), BF16),
        ((H * DH, DH), BF16),
        ((CH, DH), F32),
        ((1, DH), F32),
    )
    return pl.pallas_call(
        exchange_kernel,
        out_shape=tuple(pltpu.VMEM(s, t) for s, t in shapes),
        in_specs=[hbm] * 12,
        out_specs=(vmem,) * 12,
        scratch_shapes=[
            pltpu.SMEM((NR,), jnp.int32),
            pltpu.SMEM((1, NR), jnp.int32),
            pltpu.SMEM((NR,), jnp.int32),
            pltpu.VMEM((1, H, PIECE), F32),
            pltpu.VMEM((NR, RMAX, H * DH), BF16),
            pltpu.VMEM((NR, RMAX, H * DH), BF16),
            pltpu.VMEM((NR, H, RMAX), F32),
            pltpu.VMEM((NR, RMAX), jnp.int32),
            pltpu.VMEM((NR * 4, CH), F32),
            pltpu.VMEM((NR, H, DH, DH), BF16),
            pltpu.VMEM((PLANE, 8, DH), BF16),
            pltpu.VMEM((PLANE, 8, DH), BF16),
            pltpu.VMEM((1, DH), F32),
            pltpu.VMEM((PLANE, 1, DH), F32),
            pltpu.VMEM((32, DH), BF16),
            pltpu.VMEM((RING, 32, DH), BF16),
            pltpu.VMEM((PLANE, 32, DH), BF16),
            pltpu.VMEM((PLANE, 32, DH), BF16),
            pltpu.VMEM((PLANE, 32, DH), BF16),
            pltpu.VMEM((PLANE, 32, DH), BF16),
            pltpu.VMEM((RING, 32, DH), BF16),
            pltpu.VMEM((RING, 32, DH), BF16),
            pltpu.VMEM((4, 8, DH), BF16),
            pltpu.VMEM((PLANE, 8, DH), BF16),
            pltpu.VMEM((PLANE * 32, 2 * DH), BF16),
            pltpu.VMEM((2 * DH, PLANE * 32), BF16),
            pltpu.SemaphoreType.DMA((12,)),
            pltpu.SemaphoreType.DMA((7,)),
            pltpu.SemaphoreType.DMA((7,)),
        ],
        compiler_params=pltpu.CompilerParams(
            collective_id=0, has_side_effects=True, vmem_limit_bytes=32 << 20
        ),
        name="exchange",
    )(*args)


def finish_kernel(
    pk, pv, q, go, pout, pdq, dk, dv, starts, gfin, cols_ref, pfac,
    out_hbm, dq_hbm, dk_hbm, dv_hbm, pdk_hbm, pdv_hbm, out, dq, pdk, pdv, sems,
):
    early = [
        pltpu.make_async_copy(dk, dk_hbm, sems.at[0]),
        pltpu.make_async_copy(dv, dv_hbm, sems.at[1]),
    ]
    for c in early:
        c.start()
    cols = cols_ref[...]
    for r in range(NR):
        for h in range(H):
            hs = HEADS[h]
            state = starts[r, hs, :]
            for c, t in enumerate(TOKENS):
                e = col(cols, r, 12 + 2 * c + h)
                out[r, t, hs] = (pout[r, t, hs] + e * mm(q[r, t, hs], state, 1, 0)).astype(BF16)
                dq[r, t, hs] = (pdq[r, t, hs] + e * mm(go[r, t, hs], state, 1, 1)).astype(BF16)
        for i, (s, d) in enumerate(((out, out_hbm), (dq, dq_hbm))):
            c = pltpu.make_async_copy(s.at[r], d.at[r], sems.at[2 + 2 * r + i])
            c.start()
            early.append(c)
    for h in range(H):
        hs = HEADS[h]
        factor = cols[:, 64 + h : 65 + h] * pfac[:, h : h + 1]
        g = gfin[hs, :]
        pdk[0, :, hs] = (factor * mm(pv[0, :, hs], g, 1, 1)).astype(BF16)
        pdv[0, :, hs] = (factor * mm(pk[0, :, hs], g, 1, 0)).astype(BF16)
    for i, (s, d) in enumerate(((pdk, pdk_hbm), (pdv, pdv_hbm))):
        c = pltpu.make_async_copy(s, d, sems.at[10 + i])
        c.start()
        early.append(c)
    for c in early:
        c.wait()


def finish(*parts):
    vmem = pl.BlockSpec(memory_space=pltpu.VMEM)
    hbm = pl.BlockSpec(memory_space=pltpu.HBM)
    big = jax.ShapeDtypeStruct((NR, RMAX, H * DH), BF16)
    small = jax.ShapeDtypeStruct((1, PIECE, H * DH), BF16)
    return pl.pallas_call(
        finish_kernel,
        out_shape=(big,) * 4 + (small,) * 2,
        in_specs=[vmem] * 12,
        out_specs=(hbm,) * 6,
        scratch_shapes=[
            pltpu.VMEM((NR, RMAX, H * DH), BF16),
            pltpu.VMEM((NR, RMAX, H * DH), BF16),
            pltpu.VMEM((1, PIECE, H * DH), BF16),
            pltpu.VMEM((1, PIECE, H * DH), BF16),
            pltpu.SemaphoreType.DMA((12,)),
        ],
        compiler_params=pltpu.CompilerParams(vmem_limit_bytes=24 << 20),
        name="finish",
    )(*parts)


def shards(pk, pv, pg, q, k, v, rg, cot, gid, lens, mask, adv):
    parts = exchange(*[pltpu.with_memory_space_constraint(x, pltpu.HBM) for x in (gid, lens, adv, pk, pv, pg, q, k, v, cot, rg, mask)])
    return finish(*parts)


def solution(mesh):
    both = ("prompt", "resp")
    pieces = P("resp", "prompt", None)
    slots = P(both, None, None)
    return jax.shard_map(
        shards,
        mesh=mesh,
        in_specs=(
            pieces,
            pieces,
            P("resp", None, "prompt"),
            slots,
            slots,
            slots,
            slots,
            slots,
            P(both),
            P(both, None),
            P(both, None),
            P(both),
        ),
        out_specs=(slots, slots, slots, slots, pieces, pieces),
        check_vma=False,
    )
```
